32 devices in a mesh: dp: 8 (over y, x, core), tensor: 4 (over z).
Axes of the slice: x: 2, y: 2, z: 4, core: 2. Of those that a mesh axis runs over, the one named last changes fastest.
Arguments:
- tokens_in: bfloat16 [16, 1024, 768], P('dp', 'tensor'), may hold values from -6 to 6
- segment_ids: int32 [16, 1024], P('dp'), may hold values from 0 to 2, never falling along the last dimension, each value on 1 to 800 neighbouring positions
- timesteps: int32 [16], P('dp'), may hold values from 0 to 1999
- cotangent: bfloat16 [16, 1024, 768], P('dp', 'tensor'), may hold values from -6 to 6
- qkv_weight: bfloat16 [3, 768, 768], P(None, 'dp', 'tensor'), may hold values from -0.21875 to 0.21875
- q_bias: bfloat16 [768], P('tensor'), may hold values from -1.75 to 1.75
- v_bias: bfloat16 [768], P('tensor'), may hold values from -1.75 to 1.75
- out_weight: bfloat16 [768, 768], P('tensor', 'dp'), may hold values from -1.75 to 1.75
- out_bias: bfloat16 [768], P('dp'), may hold values from -1.75 to 1.75
- ln1_gain: bfloat16 [768], P('dp'), may hold values from 0.5 to 1.5
- ln1_bias: bfloat16 [768], P('dp'), may hold values from -1.75 to 1.75
- ffn_in_weight: bfloat16 [768, 3072], P('dp', 'tensor'), may hold values from -0.21875 to 0.21875
- ffn_in_bias: bfloat16 [3072], P('tensor'), may hold values from -1.75 to 1.75
- ffn_out_weight: bfloat16 [3072, 768], P('tensor', 'dp'), may hold values from -0.109375 to 0.109375
- ffn_out_bias: bfloat16 [768], P('dp'), may hold values from -1.75 to 1.75
- ln2_gain: bfloat16 [768], P('dp'), may hold values from 0.5 to 1.5
- ln2_bias: bfloat16 [768], P('dp'), may hold values from -1.75 to 1.75
- time_weight1: bfloat16 [128, 768], P(None, 'dp'), may hold values from -0.5 to 0.5
- time_bias1: bfloat16 [768], P('dp'), may hold values from -1.75 to 1.75
- time_weight2: bfloat16 [768, 768], P('dp'), may hold values from -0.21875 to 0.21875
- time_bias2: bfloat16 [768], P('dp'), may hold values from -1.75 to 1.75
Outputs:
- output: bfloat16 [16, 1024, 768], P('dp', 'tensor')
- input_grad: bfloat16 [16, 1024, 768], P('dp', 'tensor')
- qkv_weight_grad: float32 [3, 768, 768], P(None, 'dp', 'tensor')
- q_bias_grad: float32 [768], P('tensor')
- v_bias_grad: float32 [768], P('tensor')
- out_weight_grad: float32 [768, 768], P('tensor', 'dp')
- out_bias_grad: float32 [768], P('dp')
- ln1_gain_grad: float32 [768], P('dp')
- ln1_bias_grad: float32 [768], P('dp')
- ffn_in_weight_grad: float32 [768, 3072], P('dp', 'tensor')
- ffn_in_bias_grad: float32 [3072], P('tensor')
- ffn_out_weight_grad: float32 [3072, 768], P('tensor', 'dp')
- ffn_out_bias_grad: float32 [768], P('dp')
- ln2_gain_grad: float32 [768], P('dp')
- ln2_bias_grad: float32 [768], P('dp')
- time_weight1_grad: float32 [128, 768], P(None, 'dp')
- time_bias1_grad: float32 [768], P('dp')
- time_weight2_grad: float32 [768, 768], P('dp')
- time_bias2_grad: float32 [768], P('dp')
The draws below stay inside these ranges and needn't reach their ends.
Inputs may be any that keep to these rules, and one draw needn't show every extreme that they name: `segment_ids`: within a sequence the ids never fall; each of the 3 ids covers 1 to 800 consecutive tokens.
All inputs are finite; a program needn't handle non-finite values.
Results may differ from the reference program's by a relative error of at most 0.02.
Values may be sent and summed in bfloat16 or wider, within the bound.
No kernel may reach another device: no remote copies, remote signals or barrier semaphores. Data moves between devices by JAX's collectives and lax.ppermute only.
A program may use at most 192 MiB of HBM per device.

```python
import math
import jax
import jax.numpy as jnp
import numpy as np
from jax import lax

D = 768
H = 12
HD = 64
FF = 3072
TE = 128
SEQ = 1024
SEGS = 3
DOC_MAX = 800
STEPS = 2000
SEQS = 16


def set_ends(array, key, low, top_value):
    shape = array.shape
    place = [jax.random.randint(jax.random.fold_in(key, axis), (), 0, shape[axis]) for axis in range(len(shape))]
    array = array.at[tuple(place)].set(low)
    longest = shape.index(max(shape))
    place[longest] = (place[longest] + 1) % shape[longest]
    return array.at[tuple(place)].set(top_value)


def raised(entries, rng, source, target, shards_of, factor):
    def block_of(axis_at):
        return (jnp.arange(entries.shape[axis_at]) // (entries.shape[axis_at] // shards_of)).reshape((-1,) + (1,) * (entries.ndim - 1 - axis_at))

    one_side = jax.random.permutation(rng, shards_of)[block_of(target)]
    second = (block_of(target) + shards_of // 2) % shards_of
    return jnp.where((block_of(source) == one_side) | (block_of(source) == second), factor * entries, entries)


def level_of(rng, dims, pieces, least, high):
    loudness = 1.0
    for axis_at, blocks in pieces:
        steps = jax.random.uniform(jax.random.fold_in(jax.random.fold_in(rng, 6), axis_at), (blocks,), jnp.float32, least / len(pieces), high / len(pieces))
        loudness = loudness * jnp.repeat(jnp.exp(steps), dims[axis_at] // blocks).reshape((-1,) + (1,) * (len(dims) - 1 - axis_at))
    return loudness


def length_profile(number_of, total, bound, skew):
    weights = [(1 << 20) // math.isqrt(rank ** skew) + 1 for rank in range(2, number_of + 1)]
    rest, given = total - bound - (number_of - 1), [1] * (number_of - 1)
    while rest > 0:
        free = [i for i in range(number_of - 1) if given[i] < bound]
        whole, budget = sum([weights[i] for i in free]), rest
        for i in free:
            more = min(bound - given[i], max(1, budget * weights[i] // whole), rest)
            given[i] = given[i] + more
            rest = rest - more
    return np.array([bound] + given)


def ragged_sizes(stream_key, count, total, bound, lean):
    if count == 2:
        one = jax.random.randint(stream_key, (), max(1, total - bound), min(bound, total - 1) + 1)
        return jnp.stack([one, total - one])
    tallies = jnp.asarray(length_profile(count, total, bound, lean), jnp.int32)
    pairs = (count - 1) // 2
    donor, taker = tallies[1:1 + 2 * pairs:2], tallies[2:2 + 2 * pairs:2]
    slack = jnp.minimum(donor - 1, bound - taker)
    shifted = jax.random.randint(jax.random.fold_in(stream_key, 1), (pairs,), 0, 1 << 20) % (slack + 1)
    tallies = tallies.at[1:1 + 2 * pairs:2].set(donor - shifted).at[2:2 + 2 * pairs:2].set(taker + shifted)
    return tallies[jax.random.permutation(jax.random.fold_in(stream_key, 2), count)]


def gaussian(own_key, shape, scale, reach, split=(), kind=jnp.bfloat16):
    array = scale * jax.random.normal(own_key, shape, jnp.float32)
    if split:
        array = array * level_of(own_key, shape, split, -0.22, 0.18)
    return jnp.clip(array, -reach, reach).astype(kind)


def heavy_noise(own_key, extent, spread, bound, split, heavy, held_as=jnp.bfloat16):
    values = spread * jax.random.normal(own_key, extent, jnp.float32)
    if split:
        values = values * level_of(own_key, extent, split, -0.22, 0.18)
    return jnp.clip(raised(values, jax.random.fold_in(own_key, 3), *heavy), -bound, bound).astype(held_as)


def setup_inputs(seed: int = 0) -> dict:
    seeds = jax.random.split(jax.random.key(seed), 22)
    return {
        "tokens_in": gaussian(seeds[0], (SEQS, SEQ, D), 1.0, 6.0, ((0, 8), (1, 4))),
        "segment_ids": jax.vmap(lambda own: jnp.searchsorted(jnp.cumsum(ragged_sizes(own, SEGS, SEQ, DOC_MAX, 1)), jnp.arange(SEQ), side="right"))(jax.random.split(seeds[1], SEQS)).reshape((SEQS, SEQ)).astype(jnp.int32),
        "timesteps": set_ends(jax.random.randint(seeds[2], (SEQS,), 0, STEPS), jax.random.fold_in(seeds[2], 1), 0, STEPS - 1).astype(jnp.int32),
        "cotangent": heavy_noise(seeds[3], (SEQS, SEQ, D), 1.0, 6.0, ((0, 8), (1, 4)), (0, 2, 8, 2.0)),
        "qkv_weight": gaussian(seeds[4], (3, D, D), D ** -0.5, 0.21875, ((1, 8), (2, 4))),
        "q_bias": gaussian(seeds[5], (D,), 0.3, 1.75, ((0, 4),)),
        "v_bias": gaussian(seeds[6], (D,), 0.3, 1.75, ((0, 4),)),
        "out_weight": gaussian(seeds[7], (D, D), (D // 64) ** -0.5, 1.75, ((0, 4), (1, 8))),
        "out_bias": gaussian(seeds[8], (D,), 0.3, 1.75, ((0, 8),)),
        "ln1_gain": jnp.clip(1.0 + 0.1 * jax.random.normal(seeds[9], (D,), jnp.float32), 0.5, 1.5).astype(jnp.bfloat16),
        "ln1_bias": gaussian(seeds[10], (D,), 0.3, 1.75, ((0, 8),)),
        "ffn_in_weight": gaussian(seeds[11], (D, FF), D ** -0.5, 0.21875, ((0, 8), (1, 4))),
        "ffn_in_bias": gaussian(seeds[12], (FF,), 0.3, 1.75, ((0, 4),)),
        "ffn_out_weight": gaussian(seeds[13], (FF, D), FF ** -0.5, 0.109375, ((0, 4), (1, 8))),
        "ffn_out_bias": gaussian(seeds[14], (D,), 0.3, 1.75, ((0, 8),)),
        "ln2_gain": jnp.clip(1.0 + 0.1 * jax.random.normal(seeds[15], (D,), jnp.float32), 0.5, 1.5).astype(jnp.bfloat16),
        "ln2_bias": gaussian(seeds[16], (D,), 0.3, 1.75, ((0, 8),)),
        "time_weight1": gaussian(seeds[17], (TE, D), TE ** -0.5, 0.5, ((1, 8),)),
        "time_bias1": gaussian(seeds[18], (D,), 0.3, 1.75, ((0, 8),)),
        "time_weight2": gaussian(seeds[19], (D, D), D ** -0.5, 0.21875, ((0, 8),)),
        "time_bias2": gaussian(seeds[20], (D,), 0.3, 1.75, ((0, 8),)),
    }


@jax.custom_vjp
def low(v):
    return lax.optimization_barrier(v.astype(jnp.bfloat16)).astype(jnp.float32)

@jax.custom_vjp
def low_back(v):
    return v

def low_keep(v):
    return (low(v), None)

def low_pass(kept, grad):
    return (grad,)

def back_keep(v):
    return (v, None)

def back_low(kept, grad):
    return (low(grad),)
low.defvjp(low_keep, low_pass)
low_back.defvjp(back_keep, back_low)
epsilon = 1e-05
highest = lax.Precision.HIGHEST

def matmul_high(left_side, right_side):
    return jnp.dot(left_side, right_side, precision=highest, preferred_element_type=jnp.float32)

def step_features(step_values, width):
    half_width = width // 2
    frequency = jnp.exp(-math.log(10000.0) * jnp.arange(half_width).astype(jnp.float32) / half_width)
    angles = step_values.astype(jnp.float32)[:, None] * frequency[None, :]
    return jnp.concatenate([jnp.sin(angles), jnp.cos(angles)], axis=-1)

def time_embed(features, weight_one, shift_one, weight_two, shift_two):
    hidden_time = jax.nn.silu(matmul_high(features, weight_one) + shift_one)
    return matmul_high(hidden_time, weight_two) + shift_two

def layer_norm(values_in, norm_gain, norm_shift):
    centered = values_in - lax.optimization_barrier(jnp.mean(values_in, axis=-1, keepdims=True))
    variance = lax.optimization_barrier(jnp.mean(centered * centered, axis=-1, keepdims=True))
    return centered * lax.rsqrt(variance + epsilon) * norm_gain + norm_shift

def one_sequence(params, tokens_seq, seg_row, step_value):
    qkv_weight, q_bias, v_bias, out_weight, out_bias, ln1_gain, ln1_bias, ffn_in_weight, ffn_in_bias, ffn_out_weight, ffn_out_bias, ln2_gain, ln2_bias, time_weight1, time_bias1, time_weight2, time_bias2 = params
    scale = HD ** (-0.5)
    embedded = time_embed(step_features(step_value[None], TE), time_weight1, time_bias1, time_weight2, time_bias2)
    start = tokens_seq + embedded
    start_low = low(start)
    queries = low(low_back(matmul_high(start_low, qkv_weight[0]) + q_bias))
    keys_proj = low(low_back(matmul_high(start_low, qkv_weight[1])))
    values_proj = low(low_back(matmul_high(start_low, qkv_weight[2]) + v_bias))
    query_heads = queries.reshape(SEQ, H, HD)
    key_heads = keys_proj.reshape(SEQ, H, HD)
    value_heads = values_proj.reshape(SEQ, H, HD)
    scores = low_back(scale * jnp.einsum('qhd,khd->hqk', query_heads, key_heads, precision=highest))
    same_doc = seg_row[:, None] == seg_row[None, :]
    scores = jnp.where(same_doc[None], scores, -1e+30)
    row_top = lax.optimization_barrier(jnp.max(scores, axis=-1, keepdims=True))
    expo = jnp.exp(scores - row_top)
    probs = expo / lax.optimization_barrier(jnp.sum(expo, axis=-1, keepdims=True))
    context = jnp.einsum('hqk,khd->qhd', low(probs), value_heads, precision=highest).reshape(SEQ, D)
    context = low(low_back(context))
    attended = low_back(matmul_high(context, out_weight) + out_bias)
    normed_one = layer_norm(start + attended, ln1_gain, ln1_bias)
    inner = low_back(matmul_high(low(normed_one), ffn_in_weight) + ffn_in_bias)
    activated = low(jax.nn.gelu(inner, approximate=False))
    branch = low_back(matmul_high(activated, ffn_out_weight) + ffn_out_bias)
    return layer_norm(normed_one + branch, ln2_gain, ln2_bias)

def reference(tokens_in, segment_ids, timesteps, cotangent, qkv_weight, q_bias, v_bias, out_weight, out_bias, ln1_gain, ln1_bias, ffn_in_weight, ffn_in_bias, ffn_out_weight, ffn_out_bias, ln2_gain, ln2_bias, time_weight1, time_bias1, time_weight2, time_bias2):
    raw_params = (qkv_weight, q_bias, v_bias, out_weight, out_bias, ln1_gain, ln1_bias, ffn_in_weight, ffn_in_bias, ffn_out_weight, ffn_out_bias, ln2_gain, ln2_bias, time_weight1, time_bias1, time_weight2, time_bias2)
    params = tuple((entry.astype(jnp.float32) for entry in raw_params))
    inputs = tokens_in.astype(jnp.float32)

    def forward(inputs_all, params_all):

        def per_sequence(packed):
            return one_sequence(params_all, packed[0], packed[1], packed[2])
        return lax.map(jax.checkpoint(per_sequence), (inputs_all, segment_ids, timesteps))
    output, pullback = jax.vjp(forward, inputs, params)
    input_grad, grads = pullback(cotangent.astype(jnp.float32))
    return (output.astype(jnp.bfloat16), input_grad.astype(jnp.bfloat16), grads[0], grads[1], grads[2], grads[3], grads[4], grads[5], grads[6], grads[7], grads[8], grads[9], grads[10], grads[11], grads[12], grads[13], grads[14], grads[15], grads[16])
```

```python
import functools
import math

import jax
import jax.numpy as jnp
from jax import lax
from jax.experimental import pallas as pl
from jax.experimental.pallas import tpu as pltpu
from jax.sharding import Mesh, PartitionSpec as P

HD = 64
TE = 128
BF = jnp.bfloat16
F32 = jnp.float32
epsilon = 1e-05
highest = lax.Precision.HIGHEST


def nn(a, b):
    return lax.dot_general(a, b, (((1,), (0,)), ((), ())), preferred_element_type=F32)


def nt(a, b):
    return lax.dot_general(a, b, (((1,), (1,)), ((), ())), preferred_element_type=F32)


def tn(a, b):
    return lax.dot_general(a, b, (((0,), (0,)), ((), ())), preferred_element_type=F32)


def matmul_high(a, b):
    return jnp.dot(a, b, precision=highest, preferred_element_type=F32)


def step_features(step_values):
    half = TE // 2
    frequency = jnp.exp(-math.log(10000.0) * jnp.arange(half).astype(F32) / half)
    angles = step_values.astype(F32)[:, None] * frequency[None, :]
    return jnp.concatenate([jnp.sin(angles), jnp.cos(angles)], axis=-1)


def attend_forward(q_ref, k_ref, v_ref, kseg_ref, qseg_ref, ctx_ref, lse_ref):
    k, v, q = k_ref[...], v_ref[...], q_ref[...]
    same = kseg_ref[...] == qseg_ref[...]
    lane = lax.broadcasted_iota(jnp.int32, k.shape, 1)
    total = None
    for half in range(2):
        pick = (lane < HD) if half == 0 else (lane >= HD)
        kh = jnp.where(pick, k, jnp.zeros_like(k))
        vh = jnp.where(pick, v, jnp.zeros_like(v))
        s = jnp.where(same, nt(kh, q), -1e30)
        top = jnp.max(s, axis=0, keepdims=True)
        e = jnp.exp(s - top)
        den = jnp.sum(e, axis=0, keepdims=True)
        p = (e * (1.0 / den)).astype(BF)
        part = tn(vh, p)
        total = part if total is None else total + part
        lse_ref[0, half : half + 1, :] = top + jnp.log(den)
    ctx_ref[...] = total.T.astype(BF)


def attend_backward(
    q_ref, k_ref, v_ref, g_ref, lse_ref, kseg_ref, qseg_ref, dq_ref, dk_ref, dv_ref, dk_acc, dv_acc
):
    step = pl.program_id(1)

    @pl.when(step == 0)
    def _():
        dk_acc[...] = jnp.zeros_like(dk_acc)
        dv_acc[...] = jnp.zeros_like(dv_acc)

    k, v, q, g = k_ref[...], v_ref[...], q_ref[...], g_ref[...]
    same = kseg_ref[...] == qseg_ref[...]
    lane = lax.broadcasted_iota(jnp.int32, k.shape, 1)
    lane_q = lax.broadcasted_iota(jnp.int32, q.shape, 1)
    scale = HD**-0.5
    total = None
    for half in range(2):
        pick = (lane < HD) if half == 0 else (lane >= HD)
        pick_q = (lane_q < HD) if half == 0 else (lane_q >= HD)
        kh = jnp.where(pick, k, jnp.zeros_like(k))
        vh = jnp.where(pick, v, jnp.zeros_like(v))
        qh = jnp.where(pick_q, q, jnp.zeros_like(q))
        gh = jnp.where(pick_q, g, jnp.zeros_like(g))
        s = jnp.where(same, nt(kh, q), -1e30)
        p = jnp.exp(s - lse_ref[0, half : half + 1, :])
        dp = nt(vh, g)
        dv_acc[...] += nn(p.astype(BF), gh)
        delta = jnp.sum(p * dp, axis=0, keepdims=True)
        ds = (p * (dp - delta)).astype(BF)
        dk_acc[...] += nn(ds, qh)
        part = tn(kh, ds)
        total = part if total is None else total + part
    dq_ref[...] = (total.T * scale).astype(BF)

    @pl.when(step == pl.num_programs(1) - 1)
    def _():
        dk_ref[...] = dk_acc[...].astype(BF)
        dv_ref[...] = dv_acc[...].astype(BF)


def attention_calls(seq_len, width, block):
    pairs = width // 128
    grid = (pairs, seq_len // block)
    by_query = pl.BlockSpec((block, 128), lambda i, j: (j, i))
    whole = pl.BlockSpec((seq_len, 128), lambda i, j: (0, i))
    kseg = pl.BlockSpec((seq_len, 1), lambda i, j: (0, 0))
    qseg = pl.BlockSpec((1, block), lambda i, j: (0, j))
    lse = pl.BlockSpec((1, 2, block), lambda i, j: (i, 0, j))
    full = jax.ShapeDtypeStruct((seq_len, width), BF)
    forward = pl.pallas_call(
        attend_forward,
        grid=grid,
        in_specs=[by_query, whole, whole, kseg, qseg],
        out_specs=[by_query, lse],
        out_shape=[full, jax.ShapeDtypeStruct((pairs, 2, seq_len), F32)],
        name="attend_forward",
    )
    backward = pl.pallas_call(
        attend_backward,
        grid=grid,
        in_specs=[by_query, whole, whole, by_query, lse, kseg, qseg],
        out_specs=[by_query, whole, whole],
        out_shape=[full, full, full],
        scratch_shapes=[pltpu.VMEM((seq_len, 128), F32), pltpu.VMEM((seq_len, 128), F32)],
        name="attend_backward",
    )
    return forward, backward


def norm_parts(z):
    centered = z - jnp.mean(z, axis=-1, keepdims=True)
    r = lax.rsqrt(jnp.mean(centered * centered, axis=-1, keepdims=True) + epsilon)
    return centered * r, r


def norm_backward(c, xh, r, gain):
    dxh = c * gain
    dz = r * (
        dxh
        - jnp.mean(dxh, axis=-1, keepdims=True)
        - xh * jnp.mean(dxh * xh, axis=-1, keepdims=True)
    )
    return dz, jnp.sum(c * xh, axis=0), jnp.sum(c, axis=0)


def gelu_pair(x):
    cdf = 0.5 * (1.0 + lax.erf(x * (0.5**0.5)))
    return x * cdf, cdf


def gelu_slope(x):
    cdf = 0.5 * (1.0 + lax.erf(x * (0.5**0.5)))
    return cdf + x * jnp.exp(-0.5 * x * x) * (1.0 / math.sqrt(2.0 * math.pi))


def local(
    pair_count,
    tokens_in,
    segment_ids,
    timesteps,
    cotangent,
    qkv_weight,
    q_bias,
    v_bias,
    out_weight,
    out_bias,
    ln1_gain,
    ln1_bias,
    ffn_in_weight,
    ffn_in_bias,
    ffn_out_weight,
    ffn_out_bias,
    ln2_gain,
    ln2_bias,
    time_weight1,
    time_bias1,
    time_weight2,
    time_bias2,
):
    pair_bits = pair_count.bit_length() - 1
    dp_count = 2 * pair_count
    core = lax.axis_index("core")
    place = lax.axis_index("tensor")
    pair = lax.axis_index("pair")
    dp_index = pair * 2 + core
    micro, quarter, width = tokens_in.shape
    sub = quarter // 2
    seq_len = segment_ids.shape[1]
    rows = qkv_weight.shape[1]
    shard_cols = qkv_weight.shape[2]
    units = ffn_in_bias.shape[0]
    own_width = 2 * shard_cols
    ct = ("core", "tensor")

    def swap_core(x):
        return lax.ppermute(x, "core", [(0, 1), (1, 0)])

    def axis_step(name, size, bit):
        index = {"tensor": place, "pair": pair, "core": core}[name]
        return name, [(i, i ^ (1 << bit)) for i in range(size)], (index >> bit) & 1

    step_z1 = axis_step("tensor", 4, 1)
    step_z0 = axis_step("tensor", 4, 0)
    step_core = axis_step("core", 2, 0)
    steps_pair = [axis_step("pair", pair_count, b) for b in range(pair_bits)]

    def grow(x, step, axis):
        name, perm, bit = step
        got = lax.ppermute(x, name, perm)
        return jnp.concatenate(
            [jnp.where(bit == 0, x, got), jnp.where(bit == 0, got, x)], axis=axis
        )

    def fold(x, step, axis, wire=BF):
        name, perm, bit = step
        low, high = lax.slice_in_dim(x, 0, 1, axis=axis), lax.slice_in_dim(x, 1, 2, axis=axis)
        sent = jnp.where(bit == 0, high, low).astype(wire)
        return jnp.where(bit == 0, low, high) + lax.ppermute(sent, name, perm).astype(x.dtype)

    lead = 2 + pair_bits
    transpose_ct = [
        (h * 4 + z1 * 2 + z0, z1 * 4 + h * 2 + z0)
        for h in range(2)
        for z1 in range(2)
        for z0 in range(2)
    ]

    def route(order):
        steps = [(step_z1, 1 + pair_bits), (step_z0, 0)]
        bits = list(range(pair_bits))
        for b in bits if order == 0 else bits[::-1]:
            steps.append((steps_pair[b], pair_bits - b))
        return steps

    def gather_chunk(x, order):
        x = lax.ppermute(x, ct, transpose_ct)
        x = x.reshape((1,) * lead + x.shape)
        for step, axis in route(order):
            x = grow(x, step, axis)
        return x.reshape((2, dp_count) + x.shape[lead:])

    def scatter_chunk(x, order):
        x = x.reshape((2,) * lead + (rows, x.shape[-1]))
        for step, axis in route(order)[::-1]:
            x = fold(x, step, axis)
        x = x.reshape(x.shape[lead:]).astype(BF)
        return lax.ppermute(x, ct, transpose_ct).astype(F32)

    z1, z0 = place // 2, place % 2

    def rounds():
        for r in range(4):
            r1, r0 = r // 2, r % 2
            perm = [
                (c * 4 + a * 2 + b, (a ^ r1) * 4 + 2 * c + (b ^ r0))
                for c in range(2)
                for a in range(2)
                for b in range(2)
            ]
            yield r1, r0, perm

    def bring(x):
        x = x.reshape(micro, 2, sub, width)
        blocks = [None] * 4
        for r1, r0, perm in rounds():
            j, h = z0 ^ r0, z1 ^ r1
            block = lax.dynamic_slice(x, (j, h, 0, 0), (1, 1, sub, width))[0, 0]
            blocks[r1 * 2 + r0] = lax.ppermute(block, ct, perm)
        def pick(q):
            q1, q0 = q // 2, q % 2
            first = jnp.where((q1 ^ core) == 0, 1, 0)
            second = jnp.where((q0 ^ z0) == 0, 1, 0)
            top = jnp.where(second == 1, blocks[0], blocks[1])
            bottom = jnp.where(second == 1, blocks[2], blocks[3])
            return jnp.where(first == 1, top, bottom)

        own = jnp.stack([pick(q) for q in range(4)])
        other = swap_core(own)
        return jnp.stack(
            [jnp.where(core == 0, own, other), jnp.where(core == 0, other, own)], axis=1
        ).reshape(seq_len, width)

    def send_back(own):
        result = jnp.zeros((micro, 2, sub, width), own.dtype)
        got = {}
        for r1, r0, perm in rounds():
            back = [(b, a) for a, b in perm]
            q = 2 * (core ^ r1) + (z0 ^ r0)
            block = lax.dynamic_index_in_dim(own, q, 0, keepdims=False)
            got[(r1, r0)] = lax.ppermute(block, ct, back)
        out = []
        for j in range(2):
            line = []
            for h in range(2):
                top = jnp.where((z0 ^ j) == 0, got[(0, 0)], got[(0, 1)])
                bottom = jnp.where((z0 ^ j) == 0, got[(1, 0)], got[(1, 1)])
                line.append(jnp.where((z1 ^ h) == 0, top, bottom))
            out.append(jnp.stack(line))
        return jnp.stack(out).reshape(micro, quarter, width)

    tokens = bring(tokens_in)

    seg_other = swap_core(segment_ids)
    seg_row = lax.dynamic_index_in_dim(
        jnp.where(core == z1, segment_ids, seg_other), z0, 0, keepdims=False
    )
    kseg, qseg = seg_row[:, None], seg_row[None, :]

    small = jnp.concatenate(
        [
            jnp.stack([out_bias, ln1_gain, ln1_bias, ffn_out_bias, ln2_gain, ln2_bias]).reshape(-1),
            q_bias,
            v_bias,
            ffn_in_bias,
        ]
    )
    half_cols = 2 * shard_cols
    small_rows = -(-small.shape[0] // half_cols)
    small_rows += -small_rows % 16
    small = jnp.pad(small, (0, small_rows * half_cols - small.shape[0]))
    half_units = units // 2
    in_t = ffn_in_weight
    out_t = ffn_out_weight.T
    chunk_qk = jnp.concatenate(
        [qkv_weight[0], qkv_weight[1]], axis=1
    )
    chunk_qk = jnp.concatenate([chunk_qk, small.reshape(small_rows, half_cols)], axis=0)
    chunk_vo = jnp.concatenate([qkv_weight[2], out_weight.T], axis=1)
    got_qk = gather_chunk(chunk_qk, 0)
    got_vo = gather_chunk(chunk_vo, 1)
    got_in0 = gather_chunk(in_t[:, :half_units], 0)
    got_in1 = gather_chunk(in_t[:, half_units:], 1)
    got_out0 = gather_chunk(out_t[:, :half_units], 0)
    got_out1 = gather_chunk(out_t[:, half_units:], 1)

    def columns(got, begin, size):
        piece = got[:, :, :rows, begin : begin + size].reshape(2, width, size)
        return [piece[0], piece[1]]

    w_q = jnp.concatenate(columns(got_qk, 0, shard_cols), axis=1)
    w_k = jnp.concatenate(columns(got_qk, shard_cols, shard_cols), axis=1)
    w_v = jnp.concatenate(columns(got_vo, 0, shard_cols), axis=1)
    w_o = jnp.concatenate(columns(got_vo, shard_cols, shard_cols), axis=1)
    w_qkv = jnp.concatenate([w_q, w_k, w_v], axis=1)
    w_in = jnp.concatenate(
        columns(got_in0, 0, half_units) + columns(got_in1, 0, half_units), axis=1
    )
    w_out = jnp.concatenate(
        columns(got_out0, 0, half_units) + columns(got_out1, 0, half_units), axis=1
    )
    got_small = got_qk[:, :, rows:, :].reshape(2, dp_count, small_rows * half_cols).astype(F32)
    vectors = (
        got_small[0, :, : 6 * rows].reshape(dp_count, 6, rows).transpose(1, 0, 2).reshape(6, width)
    )
    out_shift, gain_one, shift_one, ffn_shift, gain_two, shift_two = [vectors[i] for i in range(6)]
    own_q_bias = got_small[:, 0, 6 * rows : 6 * rows + shard_cols].reshape(-1)
    own_v_bias = got_small[:, 0, 6 * rows + shard_cols : 6 * rows + 2 * shard_cols].reshape(-1)
    base = 6 * rows + 2 * shard_cols
    own_in_bias = got_small[:, 0, base : base + units]
    own_in_bias = jnp.concatenate(
        [own_in_bias[:, :half_units].reshape(-1), own_in_bias[:, half_units:].reshape(-1)]
    )

    steps_all = timesteps.astype(F32).reshape((1,) * (1 + pair_bits) + (micro,))
    steps_all = grow(steps_all, step_core, pair_bits)
    for b in range(pair_bits):
        steps_all = grow(steps_all, steps_pair[b], pair_bits - 1 - b)
    features = step_features(steps_all.reshape(-1))
    hidden_in = matmul_high(features, time_weight1.astype(F32)) + time_bias1.astype(F32)
    gate = 1.0 / (1.0 + jnp.exp(-hidden_in))
    hidden = hidden_in * gate
    partial = matmul_high(hidden, time_weight2.astype(F32))
    own_shift = lax.dynamic_update_slice(
        jnp.zeros((width,), F32), time_bias2.astype(F32), (dp_index * rows,)
    )
    partial = (partial + own_shift).reshape((2,) * pair_bits + (2 * micro, width))
    for b in reversed(range(pair_bits)):
        partial = fold(partial, steps_pair[b], pair_bits - 1 - b, wire=F32)
    partial = partial.reshape(2 * micro, width)
    embedded = lax.dynamic_index_in_dim(partial + swap_core(partial), place, 0, keepdims=True)

    attend, attend_back = attention_calls(seq_len, own_width, 256)
    start = tokens.astype(F32) + embedded
    start_low = start.astype(BF)
    shift_qkv = jnp.concatenate([own_q_bias, jnp.zeros_like(own_q_bias), own_v_bias])
    projected = (nn(start_low, w_qkv) + shift_qkv).astype(BF)
    q = projected[:, :own_width] * jnp.asarray(HD**-0.5, BF)
    k = projected[:, own_width : 2 * own_width]
    v = projected[:, 2 * own_width :]
    context, lse = attend(q, k, v, kseg, qseg)
    attended = nt(context, w_o)
    attended = attended + swap_core(attended.astype(BF)).astype(F32)
    xh_one, r_one = norm_parts(start + (attended + out_shift))
    normed = xh_one * gain_one + shift_one
    normed_low = normed.astype(BF)
    inner = nn(normed_low, w_in) + own_in_bias
    activated = gelu_pair(inner)[0].astype(BF)
    branch = nt(activated, w_out)
    branch = branch + swap_core(branch.astype(BF)).astype(F32)
    xh_two, r_two = norm_parts(normed + (branch + ffn_shift))

    def own_half(x):
        x = x.reshape(4, 2, sub, width)
        return lax.dynamic_index_in_dim(x, core, 1, keepdims=False)

    output = send_back(own_half((xh_two * gain_two + shift_two).astype(BF)))

    above = bring(cotangent).astype(F32)
    final_grad, gain_two_grad, shift_two_grad = norm_backward(above, xh_two, r_two, gain_two)
    final_low = final_grad.astype(BF)
    ffn_shift_grad = jnp.sum(final_low.astype(F32), axis=0)
    inner_grad = (nn(final_low, w_out) * gelu_slope(inner)).astype(BF)
    grad_out_t = tn(final_low, activated)
    in_shift_grad = jnp.sum(inner_grad.astype(F32), axis=0)
    normed_part = nt(inner_grad, w_in)
    grad_in = tn(normed_low, inner_grad)
    normed_grad = (
        final_grad + normed_part + swap_core(normed_part.astype(BF)).astype(F32)
    )
    mid_grad, gain_one_grad, shift_one_grad = norm_backward(normed_grad, xh_one, r_one, gain_one)
    mid_low = mid_grad.astype(BF)
    out_shift_grad = jnp.sum(mid_low.astype(F32), axis=0)
    context_grad = nn(mid_low, w_o).astype(BF)
    grad_o = tn(mid_low, context)
    dq, dk, dv = attend_back(q, k, v, context_grad, lse, kseg, qseg)
    q_shift_grad = jnp.sum(dq.astype(F32), axis=0)
    v_shift_grad = jnp.sum(dv.astype(F32), axis=0)
    grad_q = tn(start_low, dq)
    grad_k = tn(start_low, dk)
    grad_v = tn(start_low, dv)
    start_part = nt(jnp.concatenate([dq, dk, dv], axis=1), w_qkv)
    sent = lax.dynamic_index_in_dim(
        start_part.astype(BF).reshape(4, 2, sub, width), 1 - core, 1, keepdims=False
    )
    start_grad = own_half(mid_grad) + own_half(start_part) + swap_core(sent).astype(F32)
    input_grad = send_back(start_grad.astype(BF))

    def to_chunk(pieces):
        return jnp.stack(pieces)

    def split_two(x, begin, size):
        return [x[:, begin : begin + size], x[:, begin + size : begin + 2 * size]]

    shard_out0 = scatter_chunk(to_chunk(split_two(grad_out_t, 0, half_units)), 0)
    shard_out1 = scatter_chunk(to_chunk(split_two(grad_out_t, units, half_units)), 1)
    shard_in0 = scatter_chunk(to_chunk(split_two(grad_in, 0, half_units)), 0)
    shard_in1 = scatter_chunk(to_chunk(split_two(grad_in, units, half_units)), 1)
    qs, ks = split_two(grad_q, 0, shard_cols), split_two(grad_k, 0, shard_cols)
    vs, os = split_two(grad_v, 0, shard_cols), split_two(grad_o, 0, shard_cols)
    shard_qk = scatter_chunk(
        to_chunk([jnp.concatenate([qs[i], ks[i]], axis=1) for i in range(2)]), 0
    )
    shard_vo = scatter_chunk(
        to_chunk([jnp.concatenate([vs[i], os[i]], axis=1) for i in range(2)]), 1
    )

    def sum_all(x, over_core=True):
        steps = [step_z0, step_z1] + steps_pair
        if over_core:
            steps = [step_core] + steps
        for name, perm, _ in steps:
            x = x + lax.ppermute(x, name, perm)
        return x

    first_core = (core == 0).astype(F32)
    in_parts = jnp.concatenate(
        [in_shift_grad[:units].reshape(2, half_units), in_shift_grad[units:].reshape(2, half_units)],
        axis=1,
    )
    tensor_part = jnp.concatenate(
        [q_shift_grad.reshape(2, shard_cols), v_shift_grad.reshape(2, shard_cols), in_parts], axis=1
    )
    tensor_rows = lax.dynamic_update_slice(
        jnp.zeros((4, tensor_part.shape[1]), F32), tensor_part, (2 * core, 0)
    )
    vector_part = first_core * jnp.stack(
        [
            out_shift_grad,
            gain_one_grad,
            shift_one_grad,
            ffn_shift_grad,
            gain_two_grad,
            shift_two_grad,
        ]
    )
    seq_count = micro * dp_count
    time_rows = lax.dynamic_update_slice(
        jnp.zeros((seq_count, width), F32),
        jnp.sum(start_grad, axis=(0, 1))[None],
        (pair * 4 + place, 0),
    )
    packed = jnp.concatenate(
        [vector_part.reshape(-1), time_rows.reshape(-1), tensor_rows.reshape(-1)]
    ).reshape(-1, 128)
    packed = sum_all(packed).reshape(-1)
    vector_sums = packed[: 6 * width].reshape(6, width)
    time_sums = packed[6 * width : (6 + seq_count) * width].reshape(seq_count, width)
    tensor_sums = lax.dynamic_index_in_dim(
        packed[(6 + seq_count) * width :].reshape(4, -1), place, 0, keepdims=False
    )
    vector_own = lax.dynamic_slice(vector_sums, (0, dp_index * rows), (6, rows))
    q_total = tensor_sums[:shard_cols]
    v_total = tensor_sums[shard_cols : 2 * shard_cols]
    in_total = tensor_sums[2 * shard_cols :]

    highest_tn = functools.partial(
        lax.dot_general, precision=highest, preferred_element_type=F32
    )
    time_two_grad = highest_tn(hidden, time_sums, (((0,), (0,)), ((), ())))
    hidden_grad = highest_tn(time_sums, time_weight2.astype(F32), (((1,), (1,)), ((), ())))
    pre_grad = hidden_grad * (gate * (1.0 + hidden_in * (1.0 - gate)))
    time_one_grad = highest_tn(features, pre_grad, (((0,), (0,)), ((), ())))
    time_shift_one = jnp.sum(pre_grad, axis=0)
    time_shift_two = lax.dynamic_slice(jnp.sum(time_sums, axis=0), (dp_index * rows,), (rows,))

    return (
        output,
        input_grad,
        jnp.stack([shard_qk[:, :shard_cols], shard_qk[:, shard_cols:], shard_vo[:, :shard_cols]]),
        q_total,
        v_total,
        shard_vo[:, shard_cols:].T,
        vector_own[0],
        vector_own[1],
        vector_own[2],
        jnp.concatenate([shard_in0, shard_in1], axis=1),
        in_total,
        jnp.concatenate([shard_out0, shard_out1], axis=1).T,
        vector_own[3],
        vector_own[4],
        vector_own[5],
        time_one_grad,
        time_shift_one,
        time_two_grad,
        time_shift_two,
    )


def solution(mesh):
    dp_count, tensor_count = mesh.devices.shape
    assert tensor_count == 4
    pair_count = dp_count // 2
    split = Mesh(
        mesh.devices.reshape(pair_count, 2, tensor_count), ("pair", "core", "tensor")
    )
    dp = ("pair", "core")
    return jax.shard_map(
        functools.partial(local, pair_count),
        mesh=split,
        in_specs=(
            P(dp, "tensor", None),
            P(dp, None),
            P(dp),
            P(dp, "tensor", None),
            P(None, dp, "tensor"),
            P("tensor"),
            P("tensor"),
            P("tensor", dp),
            P(dp),
            P(dp),
            P(dp),
            P(dp, "tensor"),
            P("tensor"),
            P("tensor", dp),
            P(dp),
            P(dp),
            P(dp),
            P(None, dp),
            P(dp),
            P(dp, None),
            P(dp),
        ),
        out_specs=(
            P(dp, "tensor", None),
            P(dp, "tensor", None),
            P(None, dp, "tensor"),
            P("tensor"),
            P("tensor"),
            P("tensor", dp),
            P(dp),
            P(dp),
            P(dp),
            P(dp, "tensor"),
            P("tensor"),
            P("tensor", dp),
            P(dp),
            P(dp),
            P(dp),
            P(None, dp),
            P(dp),
            P(dp, None),
            P(dp),
        ),
        check_vma=False,
    )
```

```python
import functools
import math

import jax
import jax.numpy as jnp
from jax import lax
from jax.experimental import pallas as pl
from jax.experimental.pallas import tpu as pltpu
from jax.sharding import Mesh, PartitionSpec as P

HD = 64
TE = 128
BF = jnp.bfloat16
F32 = jnp.float32
epsilon = 1e-05
highest = lax.Precision.HIGHEST


def nn(a, b):
    return lax.dot_general(a, b, (((1,), (0,)), ((), ())), preferred_element_type=F32)


def nt(a, b):
    return lax.dot_general(a, b, (((1,), (1,)), ((), ())), preferred_element_type=F32)


def tn(a, b):
    return lax.dot_general(a, b, (((0,), (0,)), ((), ())), preferred_element_type=F32)


def matmul_high(a, b):
    return jnp.dot(a, b, precision=highest, preferred_element_type=F32)


def step_features(step_values):
    half = TE // 2
    frequency = jnp.exp(-math.log(10000.0) * jnp.arange(half).astype(F32) / half)
    angles = step_values.astype(F32)[:, None] * frequency[None, :]
    return jnp.concatenate([jnp.sin(angles), jnp.cos(angles)], axis=-1)


def attend_forward(q_ref, k_ref, v_ref, kseg_ref, qseg_ref, ctx_ref, lse_ref):
    k, v, q = k_ref[...], v_ref[...], q_ref[...] * jnp.asarray(HD**-0.5, BF)
    same = kseg_ref[...] == qseg_ref[...]
    lane = lax.broadcasted_iota(jnp.int32, k.shape, 1)
    total = None
    for half in range(2):
        pick = (lane < HD) if half == 0 else (lane >= HD)
        kh = jnp.where(pick, k, jnp.zeros_like(k))
        vh = jnp.where(pick, v, jnp.zeros_like(v))
        s = jnp.where(same, nt(kh, q), -1e30)
        top = jnp.max(s, axis=0, keepdims=True)
        e = jnp.exp(s - top)
        den = jnp.sum(e, axis=0, keepdims=True)
        p = (e * (1.0 / den)).astype(BF)
        part = tn(vh, p)
        total = part if total is None else total + part
        lse_ref[half : half + 1, :] = top + jnp.log(den)
    ctx_ref[...] = total.T.astype(BF)


def attend_backward(
    q_ref, k_ref, v_ref, g_ref, lse_ref, kseg_ref, qseg_ref, dq_ref, dk_ref, dv_ref, dk_acc, dv_acc
):
    step = pl.program_id(0)

    @pl.when(step == 0)
    def _():
        dk_acc[...] = jnp.zeros_like(dk_acc)
        dv_acc[...] = jnp.zeros_like(dv_acc)

    k, v, g = k_ref[...], v_ref[...], g_ref[...]
    q = q_ref[...] * jnp.asarray(HD**-0.5, BF)
    same = kseg_ref[...] == qseg_ref[...]
    lane = lax.broadcasted_iota(jnp.int32, k.shape, 1)
    lane_q = lax.broadcasted_iota(jnp.int32, q.shape, 1)
    scale = HD**-0.5
    total = None
    for half in range(2):
        pick = (lane < HD) if half == 0 else (lane >= HD)
        pick_q = (lane_q < HD) if half == 0 else (lane_q >= HD)
        kh = jnp.where(pick, k, jnp.zeros_like(k))
        vh = jnp.where(pick, v, jnp.zeros_like(v))
        qh = jnp.where(pick_q, q, jnp.zeros_like(q))
        gh = jnp.where(pick_q, g, jnp.zeros_like(g))
        s = jnp.where(same, nt(kh, q), -1e30)
        p = jnp.exp(s - lse_ref[half : half + 1, :])
        dp = nt(vh, g)
        dv_acc[...] += nn(p.astype(BF), gh)
        delta = jnp.sum(p * dp, axis=0, keepdims=True)
        ds = (p * (dp - delta)).astype(BF)
        dk_acc[...] += nn(ds, qh)
        part = tn(kh, ds)
        total = part if total is None else total + part
    dq_ref[...] = (total.T * scale).astype(BF)

    @pl.when(step == pl.num_programs(0) - 1)
    def _():
        dk_ref[...] = dk_acc[...].astype(BF)
        dv_ref[...] = dv_acc[...].astype(BF)


def attention_calls(seq_len, width, block):
    pairs = width // 128
    blocks = seq_len // block
    work = seq_len * seq_len * 2

    def cost(products, heads):
        return pl.CostEstimate(
            flops=products * work * 4 * HD * heads,
            transcendentals=work * heads // 2,
            bytes_accessed=heads * seq_len * 128 * 10,
        )

    one = jax.ShapeDtypeStruct((seq_len, 128), BF)

    def forward(i):
        return pl.pallas_call(
            attend_forward,
            grid=(blocks,),
            in_specs=[
                pl.BlockSpec((block, 128), lambda j: (j, i)),
                pl.BlockSpec((seq_len, 128), lambda j: (0, pairs + i)),
                pl.BlockSpec((seq_len, 128), lambda j: (0, i)),
                pl.BlockSpec((seq_len, 1), lambda j: (0, 0)),
                pl.BlockSpec((1, block), lambda j: (0, j)),
            ],
            out_specs=[
                pl.BlockSpec((block, 128), lambda j: (j, 0)),
                pl.BlockSpec((2, block), lambda j: (0, j)),
            ],
            out_shape=[one, jax.ShapeDtypeStruct((2, seq_len), F32)],
            cost_estimate=cost(2, 2),
            name="attend_forward",
        )

    def backward(i):
        return pl.pallas_call(
            attend_backward,
            grid=(blocks,),
            in_specs=[
                pl.BlockSpec((block, 128), lambda j: (j, i)),
                pl.BlockSpec((seq_len, 128), lambda j: (0, pairs + i)),
                pl.BlockSpec((seq_len, 128), lambda j: (0, i)),
                pl.BlockSpec((block, 128), lambda j: (j, i)),
                pl.BlockSpec((2, block), lambda j: (0, j)),
                pl.BlockSpec((seq_len, 1), lambda j: (0, 0)),
                pl.BlockSpec((1, block), lambda j: (0, j)),
            ],
            out_specs=[
                pl.BlockSpec((block, 128), lambda j: (j, 0)),
                pl.BlockSpec((seq_len, 128), lambda j: (0, 0)),
                pl.BlockSpec((seq_len, 128), lambda j: (0, 0)),
            ],
            out_shape=[one, one, one],
            scratch_shapes=[pltpu.VMEM((seq_len, 128), F32), pltpu.VMEM((seq_len, 128), F32)],
            cost_estimate=cost(5, 2),
            name="attend_backward",
        )

    return [forward(i) for i in range(pairs)], [backward(i) for i in range(pairs)]


def norm_parts(z):
    centered = z - jnp.mean(z, axis=-1, keepdims=True)
    r = lax.rsqrt(jnp.mean(centered * centered, axis=-1, keepdims=True) + epsilon)
    return centered * r, r


def norm_backward(c, xh, r, gain):
    dxh = c * gain
    dz = r * (
        dxh
        - jnp.mean(dxh, axis=-1, keepdims=True)
        - xh * jnp.mean(dxh * xh, axis=-1, keepdims=True)
    )
    return dz, jnp.sum(c * xh, axis=0), jnp.sum(c, axis=0)


def gelu_pair(x):
    cdf = 0.5 * (1.0 + lax.erf(x * (0.5**0.5)))
    return x * cdf, cdf


def gelu_slope(x):
    cdf = 0.5 * (1.0 + lax.erf(x * (0.5**0.5)))
    return cdf + x * jnp.exp(-0.5 * x * x) * (1.0 / math.sqrt(2.0 * math.pi))


def local(
    pair_count,
    tokens_in,
    segment_ids,
    timesteps,
    cotangent,
    qkv_weight,
    q_bias,
    v_bias,
    out_weight,
    out_bias,
    ln1_gain,
    ln1_bias,
    ffn_in_weight,
    ffn_in_bias,
    ffn_out_weight,
    ffn_out_bias,
    ln2_gain,
    ln2_bias,
    time_weight1,
    time_bias1,
    time_weight2,
    time_bias2,
):
    pair_bits = pair_count.bit_length() - 1
    dp_count = 2 * pair_count
    core = lax.axis_index("core")
    place = lax.axis_index("tensor")
    pair = lax.axis_index("pair")
    dp_index = pair * 2 + core
    micro, quarter, width = tokens_in.shape
    sub = quarter // 2
    seq_len = segment_ids.shape[1]
    rows = qkv_weight.shape[1]
    shard_cols = qkv_weight.shape[2]
    units = ffn_in_bias.shape[0]
    own_width = 2 * shard_cols
    ct = ("core", "tensor")

    def swap_core(x):
        return lax.ppermute(x, "core", [(0, 1), (1, 0)])

    def axis_step(name, size, bit):
        index = {"tensor": place, "pair": pair, "core": core}[name]
        return name, [(i, i ^ (1 << bit)) for i in range(size)], (index >> bit) & 1

    step_z1 = axis_step("tensor", 4, 1)
    step_z0 = axis_step("tensor", 4, 0)
    step_core = axis_step("core", 2, 0)
    steps_pair = [axis_step("pair", pair_count, b) for b in range(pair_bits)]

    def grow(x, step, axis):
        name, perm, bit = step
        got = lax.ppermute(x, name, perm)
        return jnp.concatenate(
            [jnp.where(bit == 0, x, got), jnp.where(bit == 0, got, x)], axis=axis
        )

    def fold(x, step, axis, wire=BF):
        name, perm, bit = step
        sent = lax.dynamic_index_in_dim(x, 1 - bit, axis).astype(wire)
        kept = lax.dynamic_index_in_dim(x, bit, axis)
        return kept + lax.ppermute(sent, name, perm).astype(x.dtype)

    turn_perm = [
        (h * 4 + a * 2 + b, a * 4 + h * 2 + b)
        for h in range(2)
        for a in range(2)
        for b in range(2)
    ]
    z1, z0 = place // 2, place % 2

    def turn(x):
        return lax.ppermute(x, ct, turn_perm)

    def pick(x, index, axis):
        return lax.dynamic_index_in_dim(x, index, axis, keepdims=False)

    def in_order(bit, mine, got):
        return jnp.where(bit == 0, mine, got), jnp.where(bit == 0, got, mine)

    def after(x, *others):
        return lax.optimization_barrier((x, *others))[0]

    def gather_z0(x):
        return in_order(z0, x, lax.ppermute(x, *step_z0[:2]))

    def row_steps(order):
        bits = list(range(pair_bits))
        return [(steps_pair[b], pair_bits - 1 - b) for b in (bits if order == 0 else bits[::-1])]

    def scatter_start(x):
        return x.reshape((2,) * pair_bits + (2, rows, x.shape[-1]))

    def scatter_columns(x, column_pieces):
        sides = [
            jnp.concatenate(
                [
                    x[:, :, (2 * i + side) * column_pieces : (2 * i + side + 1) * column_pieces]
                    for i in range(x.shape[-1] // (2 * column_pieces))
                ],
                axis=-1,
            )
            for side in range(2)
        ]
        return fold(jnp.stack(sides), step_z0, 0)[0]

    def natural(left, right, column_pieces):
        return jnp.concatenate(
            [
                piece[..., i * column_pieces : (i + 1) * column_pieces]
                for i in range(left.shape[-1] // column_pieces)
                for piece in (left, right)
            ],
            axis=-1,
        )

    def bring_z0(x):
        got = lax.ppermute(pick(x, 1 - z0, 0), *step_z0[:2])
        return jnp.concatenate(in_order(z0, pick(x, z0, 0), got), axis=0)

    def both_cores(own):
        return jnp.concatenate(in_order(core, own, swap_core(own)), axis=0)

    def send_back(own):
        x = own.reshape(2, quarter, width)
        got = lax.ppermute(pick(x, 1 - z0, 0), *step_z0[:2])
        return turn(jnp.stack(in_order(z0, pick(x, z0, 0), got)))

    seg_other = swap_core(segment_ids)
    seg_row = lax.dynamic_index_in_dim(
        jnp.where(core == z1, segment_ids, seg_other), z0, 0, keepdims=False
    )
    kseg, qseg = seg_row[:, None], seg_row[None, :]

    def time_forward(steps_all):
        features = step_features(steps_all.reshape(-1))
        hidden_in = matmul_high(features, time_weight1.astype(F32)) + time_bias1.astype(F32)
        gate = 1.0 / (1.0 + jnp.exp(-hidden_in))
        hidden = hidden_in * gate
        partial = matmul_high(hidden, time_weight2.astype(F32))
        own_shift = lax.dynamic_update_slice(
            jnp.zeros((width,), F32), time_bias2.astype(F32), (dp_index * rows,)
        )
        partial = (partial + own_shift).reshape((2,) * pair_bits + (2 * micro, width))
        return features, hidden_in, gate, hidden, partial

    assert units == own_width * 2 and 6 * rows + shard_cols <= units
    chunk_width = units
    small = jnp.concatenate(
        [
            jnp.stack([out_bias, ln1_gain, ln1_bias, ffn_out_bias, ln2_gain, ln2_bias]).reshape(-1),
            q_bias,
            jnp.zeros((chunk_width - 6 * rows - shard_cols,), BF),
            v_bias,
            jnp.zeros((chunk_width - shard_cols,), BF),
            ffn_in_bias,
        ]
    ).reshape(3, chunk_width)
    attn_shard = jnp.concatenate(
        [qkv_weight[0], qkv_weight[1], qkv_weight[2], out_weight.T], axis=1
    )
    attn_shard = jnp.concatenate([attn_shard, jnp.pad(small, ((0, 13), (0, 0)))], axis=0)

    ts = timesteps.astype(F32).reshape((1,) * (1 + pair_bits) + (micro,))
    attn = turn(attn_shard)
    ts = grow(ts, step_core, pair_bits)
    attn, ts = lax.optimization_barrier((attn, ts))
    attn = grow(attn[None], step_z1, 0)
    ts = grow(ts, steps_pair[0], pair_bits - 1)
    attn, ts, tokens = lax.optimization_barrier((attn, ts, tokens_in))
    left, right = gather_z0(attn)
    for b in range(1, pair_bits):
        ts = grow(ts, steps_pair[b], pair_bits - 1 - b)
    tokens = turn(tokens)
    attn = jnp.concatenate(
        [
            natural(left[:, :rows], right[:, :rows], shard_cols),
            jnp.concatenate([left[:, rows:], right[:, rows:]], axis=-1),
        ],
        axis=1,
    )
    attn, ts = lax.optimization_barrier((attn, ts))
    features, hidden_in, gate, hidden, partial = time_forward(ts)
    lead = (1,) * pair_bits
    attn_a = attn[:, :, :chunk_width].reshape(lead + (2, -1, chunk_width))
    attn_b = attn[:, :, chunk_width:].reshape(lead + (2, -1, chunk_width))
    fold_steps = [(steps_pair[b], pair_bits - 1 - b) for b in reversed(range(pair_bits))]
    ffn = jnp.concatenate([ffn_in_weight, ffn_out_weight.T], axis=1)
    for index in range(pair_bits):
        attn_a = grow(attn_a, *row_steps(0)[index])
        attn_b = grow(attn_b, *row_steps(1)[index])
        partial = fold(partial, *fold_steps[index], wire=F32)
        if index == pair_bits - 2 or pair_bits == 1:
            tokens = bring_z0(tokens)
        attn_a, attn_b, partial, ffn = lax.optimization_barrier((attn_a, attn_b, partial, ffn))
        if index == 0:
            ffn = turn(ffn)
    partial = partial.reshape(2 * micro, width)
    embedded = lax.dynamic_index_in_dim(partial + swap_core(partial), place, 0, keepdims=True)
    tokens = both_cores(tokens)
    ffn, attn_a = lax.optimization_barrier((ffn, attn_a))
    ffn = grow(ffn[None], step_z1, 0)
    attn_a = attn_a.reshape((dp_count,) + attn_a.shape[pair_bits + 1 :])
    attn_b = attn_b.reshape((dp_count,) + attn_b.shape[pair_bits + 1 :])
    w_qk = attn_a[:, :rows].reshape(width, chunk_width)
    w_vo = attn_b[:, :rows].reshape(width, chunk_width)
    w_v, w_o = w_vo[:, :own_width], w_vo[:, own_width:]

    small_a = attn_a[:, rows : rows + 3].astype(F32)
    small_b = attn_b[0, rows : rows + 3].astype(F32)
    vectors = (
        small_a[:, 0, : 6 * rows].reshape(dp_count, 6, rows).transpose(1, 0, 2).reshape(6, width)
    )
    out_shift, gain_one, shift_one, ffn_shift, gain_two, shift_two = [vectors[i] for i in range(6)]
    small_z = (small_a[0], small_b)
    own_q_bias = jnp.concatenate([x[0, 6 * rows : 6 * rows + shard_cols] for x in small_z])
    own_v_bias = jnp.concatenate([x[1, :shard_cols] for x in small_z])
    own_in_bias = jnp.concatenate([x[2] for x in small_z])

    attend, attend_back = attention_calls(seq_len, own_width, 256)
    start = tokens.astype(F32) + embedded
    start_low = start.astype(BF)
    shift_qk = jnp.concatenate([own_q_bias, jnp.zeros_like(own_q_bias)])
    qk = (nn(start_low, w_qk) + shift_qk).astype(BF)
    v = (nn(start_low, w_v) + own_v_bias).astype(BF)
    ffn = after(ffn, start_low)
    ffn_left, ffn_right = gather_z0(ffn)
    ffn = natural(ffn_left, ffn_right, units)
    ahead = [attend[i](qk, qk, v, kseg, qseg) for i in range(len(attend))]
    w_in = ffn[:, :, : 2 * units].reshape(lead + (2, rows, 2 * units))
    w_out = ffn[:, :, 2 * units :].reshape(lead + (2, rows, 2 * units))
    for index in range(pair_bits):
        w_in, w_out, above = lax.optimization_barrier(
            (w_in, w_out, cotangent, ahead[min(index, len(ahead) - 1)][0])
        )[:3]
        if index == 0:
            above = turn(above)
            turned = above
        w_in = grow(w_in, *row_steps(0)[index])
        w_out = grow(w_out, *row_steps(1)[index])
    above = after(turned, ahead[-1][0])
    above = bring_z0(above)
    w_in = w_in.reshape(width, 2 * units)
    w_out = w_out.reshape(width, 2 * units)
    context = jnp.concatenate([x[0] for x in ahead], axis=1)
    attended = nt(context, w_o)
    attended = attended + swap_core(attended.astype(BF)).astype(F32)
    xh_one, r_one = norm_parts(start + (attended + out_shift))
    normed = xh_one * gain_one + shift_one
    normed_low = normed.astype(BF)
    inner = nn(normed_low, w_in) + own_in_bias
    activated = gelu_pair(inner)[0].astype(BF)
    branch = nt(activated, w_out)
    branch = branch + swap_core(branch.astype(BF)).astype(F32)
    xh_two, r_two = norm_parts(normed + (branch + ffn_shift))
    half_len = seq_len // 2

    def half_of(x, which):
        return lax.dynamic_slice_in_dim(x, which * half_len, half_len, axis=0)

    output = send_back(half_of((xh_two * gain_two + shift_two).astype(BF), core))

    above = both_cores(above).astype(F32)
    final_grad, gain_two_grad, shift_two_grad = norm_backward(above, xh_two, r_two, gain_two)
    final_low = final_grad.astype(BF)
    ffn_shift_grad = jnp.sum(final_low.astype(F32), axis=0)
    inner_grad = (nn(final_low, w_out) * gelu_slope(inner)).astype(BF)
    in_shift_grad = jnp.sum(inner_grad.astype(F32), axis=0)
    normed_part = nt(inner_grad, w_in)
    normed_other = swap_core(normed_part.astype(BF))
    rows_out = scatter_start(tn(final_low, activated))
    rows_out = fold(rows_out, *row_steps(1)[::-1][0])
    rows_in = scatter_start(tn(normed_low, inner_grad))
    rows_in = fold(rows_in, *row_steps(0)[::-1][0])
    normed_grad = final_grad + normed_part + normed_other.astype(F32)
    mid_grad, gain_one_grad, shift_one_grad = norm_backward(normed_grad, xh_one, r_one, gain_one)
    mid_low = mid_grad.astype(BF)
    out_shift_grad = jnp.sum(mid_low.astype(F32), axis=0)
    context_grad = nn(mid_low, w_o).astype(BF)
    grad_o = tn(mid_low, context)
    grads = [
        attend_back[i](qk, qk, v, context_grad, ahead[i][1], kseg, qseg)
        for i in range(len(attend_back))
    ]
    rows_in, rows_out = lax.optimization_barrier((rows_in, rows_out, grads[0][0]))[:2]
    for index in range(1, pair_bits):
        rows_out = fold(rows_out, *row_steps(1)[::-1][index])
        rows_in = fold(rows_in, *row_steps(0)[::-1][index])
    rest = jnp.concatenate(
        [x.reshape(x.shape[pair_bits:]) for x in (rows_in, rows_out)], axis=-1
    )
    rest = after(rest, grads[1][0])
    rest = scatter_columns(rest, units)
    rest = after(rest, grads[-1][0])
    rest = fold(rest, step_z1, 0)[0].astype(BF)
    dqkv = jnp.concatenate([g[i] for i in range(3) for g in grads], axis=1)
    grad_qkv = tn(start_low, dqkv)
    rows_qk = scatter_start(grad_qkv[:, :chunk_width])
    rows_vo = scatter_start(jnp.concatenate([grad_qkv[:, chunk_width:], grad_o], axis=1))
    rows_qk = fold(rows_qk, *row_steps(0)[::-1][0])
    rows_vo = fold(rows_vo, *row_steps(1)[::-1][0])
    dqkv = after(dqkv, grad_qkv)
    dqk, dv = dqkv[:, :chunk_width], dqkv[:, chunk_width:]
    q_shift_grad = jnp.sum(dqk[:, :own_width].astype(F32), axis=0)
    v_shift_grad = jnp.sum(dv.astype(F32), axis=0)
    start_part = nt(dqk, w_qk) + nt(dv, w_v)
    start_other = swap_core(half_of(start_part.astype(BF), 1 - core))
    start_grad = half_of(mid_grad, core) + half_of(start_part, core) + start_other.astype(F32)

    def sum_step(x, step):
        return x + lax.ppermute(x, *step[:2])

    first_core = (core == 0).astype(F32)
    tensor_part = jnp.concatenate(
        [
            q_shift_grad.reshape(2, shard_cols),
            v_shift_grad.reshape(2, shard_cols),
            in_shift_grad.reshape(2, units),
        ],
        axis=1,
    )
    tensor_rows = lax.dynamic_update_slice(
        jnp.zeros((4, tensor_part.shape[1]), F32), tensor_part, (2 * core, 0)
    )
    vector_part = first_core * jnp.stack(
        [
            out_shift_grad,
            gain_one_grad,
            shift_one_grad,
            ffn_shift_grad,
            gain_two_grad,
            shift_two_grad,
        ]
    )
    seq_count = micro * dp_count
    time_rows = lax.dynamic_update_slice(
        jnp.zeros((seq_count, width), F32),
        jnp.sum(start_grad, axis=0)[None],
        (pair * 4 + place, 0),
    )
    packed = jnp.concatenate(
        [vector_part.reshape(-1), time_rows.reshape(-1), tensor_rows.reshape(-1)]
    ).reshape(-1, 128)
    rows_qk, rows_vo, start_grad_low = lax.optimization_barrier(
        (rows_qk, rows_vo, start_grad.astype(BF))
    )
    packed = sum_step(packed, step_core)
    for index in range(1, pair_bits):
        rows_qk = fold(rows_qk, *row_steps(0)[::-1][index])
        rows_vo = fold(rows_vo, *row_steps(1)[::-1][index])
        packed = sum_step(packed, steps_pair[index])
        rows_qk, rows_vo, packed = lax.optimization_barrier((rows_qk, rows_vo, packed))
    shard_attn = jnp.concatenate(
        [x.reshape(x.shape[pair_bits:]) for x in (rows_qk, rows_vo)], axis=-1
    )
    shard_attn = scatter_columns(shard_attn, shard_cols)
    packed = sum_step(packed, steps_pair[0])
    shard_attn, packed = lax.optimization_barrier((shard_attn, packed))
    shard_attn = fold(shard_attn, step_z1, 0)[0].astype(BF)
    packed = sum_step(packed, step_z1)
    shard_attn, packed, rest = lax.optimization_barrier((shard_attn, packed, rest))
    finished = turn(jnp.concatenate([rest, shard_attn], axis=1)).astype(F32)
    shard_ffn, shard_attn = finished[:, : 2 * units], finished[:, 2 * units :]
    packed = sum_step(packed, step_z0).reshape(-1)
    input_grad = send_back(start_grad_low)
    vector_sums = packed[: 6 * width].reshape(6, width)
    time_sums = packed[6 * width : (6 + seq_count) * width].reshape(seq_count, width)
    tensor_sums = lax.dynamic_index_in_dim(
        packed[(6 + seq_count) * width :].reshape(4, -1), place, 0, keepdims=False
    )
    vector_own = lax.dynamic_slice(vector_sums, (0, dp_index * rows), (6, rows))
    q_total = tensor_sums[:shard_cols]
    v_total = tensor_sums[shard_cols : 2 * shard_cols]
    in_total = tensor_sums[2 * shard_cols :]

    highest_tn = functools.partial(
        lax.dot_general, precision=highest, preferred_element_type=F32
    )
    time_two_grad = highest_tn(hidden, time_sums, (((0,), (0,)), ((), ())))
    hidden_grad = highest_tn(time_sums, time_weight2.astype(F32), (((1,), (1,)), ((), ())))
    pre_grad = hidden_grad * (gate * (1.0 + hidden_in * (1.0 - gate)))
    time_one_grad = highest_tn(features, pre_grad, (((0,), (0,)), ((), ())))
    time_shift_one = jnp.sum(pre_grad, axis=0)
    time_shift_two = lax.dynamic_slice(jnp.sum(time_sums, axis=0), (dp_index * rows,), (rows,))

    return (
        output,
        input_grad,
        jnp.stack([shard_attn[:, i * shard_cols : (i + 1) * shard_cols] for i in range(3)]),
        q_total,
        v_total,
        shard_attn[:, 3 * shard_cols :].T,
        vector_own[0],
        vector_own[1],
        vector_own[2],
        shard_ffn[:, :units],
        in_total,
        shard_ffn[:, units:].T,
        vector_own[3],
        vector_own[4],
        vector_own[5],
        time_one_grad,
        time_shift_one,
        time_two_grad,
        time_shift_two,
    )


def solution(mesh):
    dp_count, tensor_count = mesh.devices.shape
    assert tensor_count == 4
    pair_count = dp_count // 2
    split = Mesh(
        mesh.devices.reshape(pair_count, 2, tensor_count), ("pair", "core", "tensor")
    )
    dp = ("pair", "core")
    return jax.shard_map(
        functools.partial(local, pair_count),
        mesh=split,
        in_specs=(
            P(dp, "tensor", None),
            P(dp, None),
            P(dp),
            P(dp, "tensor", None),
            P(None, dp, "tensor"),
            P("tensor"),
            P("tensor"),
            P("tensor", dp),
            P(dp),
            P(dp),
            P(dp),
            P(dp, "tensor"),
            P("tensor"),
            P("tensor", dp),
            P(dp),
            P(dp),
            P(dp),
            P(None, dp),
            P(dp),
            P(dp, None),
            P(dp),
        ),
        out_specs=(
            P(dp, "tensor", None),
            P(dp, "tensor", None),
            P(None, dp, "tensor"),
            P("tensor"),
            P("tensor"),
            P("tensor", dp),
            P(dp),
            P(dp),
            P(dp),
            P(dp, "tensor"),
            P("tensor"),
            P("tensor", dp),
            P(dp),
            P(dp),
            P(dp),
            P(None, dp),
            P(dp),
            P(dp, None),
            P(dp),
        ),
        check_vma=False,
    )
```

```python
import functools
import math

import jax
import jax.numpy as jnp
from jax import lax
from jax.experimental import pallas as pl
from jax.experimental.pallas import tpu as pltpu
from jax.sharding import Mesh, PartitionSpec as P


HD = 64
TE = 128
BF = jnp.bfloat16
F32 = jnp.float32
epsilon = 1e-05
highest = lax.Precision.HIGHEST


def nn(a, b):
    return lax.dot_general(a, b, (((1,), (0,)), ((), ())), preferred_element_type=F32)


def nt(a, b):
    return lax.dot_general(a, b, (((1,), (1,)), ((), ())), preferred_element_type=F32)


def tn(a, b):
    return lax.dot_general(a, b, (((0,), (0,)), ((), ())), preferred_element_type=F32)


def matmul_high(a, b):
    return jnp.dot(a, b, precision=highest, preferred_element_type=F32)


def step_features(step_values):
    half = TE // 2
    frequency = jnp.exp(-math.log(10000.0) * jnp.arange(half).astype(F32) / half)
    angles = step_values.astype(F32)[:, None] * frequency[None, :]
    return jnp.concatenate([jnp.sin(angles), jnp.cos(angles)], axis=-1)


def attend_forward(q_ref, k_ref, v_ref, kseg_ref, qseg_ref, *refs):
    ctx_ref, lse_ref = refs[-2:]
    k, v, q = k_ref[...], v_ref[...], q_ref[...] * jnp.asarray(HD**-0.5, BF)
    same = kseg_ref[...] == qseg_ref[...]
    lane = lax.broadcasted_iota(jnp.int32, k.shape, 1)
    total = None
    for half in range(2):
        pick = (lane < HD) if half == 0 else (lane >= HD)
        kh = jnp.where(pick, k, jnp.zeros_like(k))
        vh = jnp.where(pick, v, jnp.zeros_like(v))
        s = jnp.where(same, nt(kh, q), -1e30)
        top = jnp.max(s, axis=0, keepdims=True)
        e = jnp.exp(s - top)
        den = jnp.sum(e, axis=0, keepdims=True)
        p = (e * (1.0 / den)).astype(BF)
        part = tn(vh, p)
        total = part if total is None else total + part
        lse_ref[half : half + 1, :] = top + jnp.log(den)
    ctx_ref[...] = total.T.astype(BF)


def attend_backward(
    q_ref, k_ref, v_ref, g_ref, lse_ref, kseg_ref, qseg_ref, out_ref, dk_acc, dv_acc
):
    step = pl.program_id(0)

    @pl.when(step == 0)
    def _():
        dk_acc[...] = jnp.zeros_like(dk_acc)
        dv_acc[...] = jnp.zeros_like(dv_acc)

    k, v, g = k_ref[...], v_ref[...], g_ref[...]
    q = q_ref[...] * jnp.asarray(HD**-0.5, BF)
    same = kseg_ref[...] == qseg_ref[...]
    lane = lax.broadcasted_iota(jnp.int32, k.shape, 1)
    lane_q = lax.broadcasted_iota(jnp.int32, q.shape, 1)
    scale = HD**-0.5
    total = None
    for half in range(2):
        pick = (lane < HD) if half == 0 else (lane >= HD)
        pick_q = (lane_q < HD) if half == 0 else (lane_q >= HD)
        kh = jnp.where(pick, k, jnp.zeros_like(k))
        vh = jnp.where(pick, v, jnp.zeros_like(v))
        qh = jnp.where(pick_q, q, jnp.zeros_like(q))
        gh = jnp.where(pick_q, g, jnp.zeros_like(g))
        s = jnp.where(same, nt(kh, q), -1e30)
        p = jnp.exp(s - lse_ref[half : half + 1, :])
        dp = nt(vh, g)
        dv_acc[...] += nn(p.astype(BF), gh)
        delta = jnp.sum(p * dp, axis=0, keepdims=True)
        ds = (p * (dp - delta)).astype(BF)
        dk_acc[...] += nn(ds, qh)
        part = tn(kh, ds)
        total = part if total is None else total + part
    block = q.shape[0]
    out_ref[pl.ds(pl.multiple_of(step * block, block), block), :128] = (total.T * scale).astype(BF)

    @pl.when(step == pl.num_programs(0) - 1)
    def _():
        out_ref[:, 128:256] = dk_acc[...].astype(BF)
        out_ref[:, 256:] = dv_acc[...].astype(BF)


def attention_calls(seq_len, width, block):
    pairs = width // 128
    blocks = seq_len // block
    work = seq_len * seq_len * 2

    def cost(products, heads):
        return pl.CostEstimate(
            flops=products * work * 4 * HD * heads,
            transcendentals=work * heads // 2,
            bytes_accessed=heads * seq_len * 128 * 10,
        )

    whole = jax.ShapeDtypeStruct((seq_len, width), BF)

    def forward(i):
        return pl.pallas_call(
            attend_forward,
            grid=(blocks,),
            in_specs=[
                pl.BlockSpec((block, 128), lambda j: (j, i)),
                pl.BlockSpec((seq_len, 128), lambda j: (0, pairs + i)),
                pl.BlockSpec((seq_len, 128), lambda j: (0, i)),
                pl.BlockSpec((seq_len, 1), lambda j: (0, 0)),
                pl.BlockSpec((1, block), lambda j: (0, j)),
            ]
            + ([pl.BlockSpec(memory_space=pl.ANY)] if i else []),
            out_specs=[
                pl.BlockSpec((block, 128), lambda j: (j, i)),
                pl.BlockSpec((2, block), lambda j: (0, j)),
            ],
            out_shape=[whole, jax.ShapeDtypeStruct((2, seq_len), F32)],
            cost_estimate=cost(2, 2),
            input_output_aliases={5: 0} if i else {},
            name="attend_forward",
        )

    def backward(i):
        return pl.pallas_call(
            attend_backward,
            grid=(blocks,),
            in_specs=[
                pl.BlockSpec((block, 128), lambda j: (j, i)),
                pl.BlockSpec((seq_len, 128), lambda j: (0, pairs + i)),
                pl.BlockSpec((seq_len, 128), lambda j: (0, i)),
                pl.BlockSpec((block, 128), lambda j: (j, i)),
                pl.BlockSpec((2, block), lambda j: (0, j)),
                pl.BlockSpec((seq_len, 1), lambda j: (0, 0)),
                pl.BlockSpec((1, block), lambda j: (0, j)),
            ],
            out_specs=pl.BlockSpec((seq_len, 384), lambda j: (0, 0)),
            out_shape=jax.ShapeDtypeStruct((seq_len, 384), BF),
            scratch_shapes=[pltpu.VMEM((seq_len, 128), F32), pltpu.VMEM((seq_len, 128), F32)],
            cost_estimate=cost(5, 2),
            name="attend_backward",
        )

    return [forward(i) for i in range(pairs)], [backward(i) for i in range(pairs)]


def norm_parts(z):
    centered = z - jnp.mean(z, axis=-1, keepdims=True)
    r = lax.rsqrt(jnp.mean(centered * centered, axis=-1, keepdims=True) + epsilon)
    return centered * r, r


def norm_backward(c, xh, r, gain):
    dxh = c * gain
    dz = r * (
        dxh
        - jnp.mean(dxh, axis=-1, keepdims=True)
        - xh * jnp.mean(dxh * xh, axis=-1, keepdims=True)
    )
    return dz, jnp.sum(c * xh, axis=0), jnp.sum(c, axis=0)


def gelu_pair(x):
    cdf = 0.5 * (1.0 + lax.erf(x * (0.5**0.5)))
    return x * cdf, cdf


def gelu_slope(x):
    cdf = 0.5 * (1.0 + lax.erf(x * (0.5**0.5)))
    return cdf + x * jnp.exp(-0.5 * x * x) * (1.0 / math.sqrt(2.0 * math.pi))


def local(
    pair_count,
    tokens_in,
    segment_ids,
    timesteps,
    cotangent,
    qkv_weight,
    q_bias,
    v_bias,
    out_weight,
    out_bias,
    ln1_gain,
    ln1_bias,
    ffn_in_weight,
    ffn_in_bias,
    ffn_out_weight,
    ffn_out_bias,
    ln2_gain,
    ln2_bias,
    time_weight1,
    time_bias1,
    time_weight2,
    time_bias2,
):
    pair_bits = pair_count.bit_length() - 1
    dp_count = 2 * pair_count
    core = lax.axis_index("core")
    place = lax.axis_index("tensor")
    pair = lax.axis_index("pair")
    dp_index = pair * 2 + core
    micro, quarter, width = tokens_in.shape
    seq_len = segment_ids.shape[1]
    rows = qkv_weight.shape[1]
    shard_cols = qkv_weight.shape[2]
    units = ffn_in_bias.shape[0]
    own_width = 2 * shard_cols
    ct = ("core", "tensor")

    def swap_core(x):
        return lax.ppermute(x, "core", [(0, 1), (1, 0)])

    def axis_step(name, size, bit):
        index = {"tensor": place, "pair": pair, "core": core}[name]
        return name, [(i, i ^ (1 << bit)) for i in range(size)], (index >> bit) & 1

    step_z1 = axis_step("tensor", 4, 1)
    step_z0 = axis_step("tensor", 4, 0)
    step_core = axis_step("core", 2, 0)
    steps_pair = [axis_step("pair", pair_count, b) for b in range(pair_bits)]

    def grow(x, step, axis):
        name, perm, bit = step
        got = lax.ppermute(x, name, perm)
        return jnp.concatenate(
            [jnp.where(bit == 0, x, got), jnp.where(bit == 0, got, x)], axis=axis
        )

    def fold(x, step, axis, wire=BF):
        name, perm, bit = step
        sent = lax.dynamic_index_in_dim(x, 1 - bit, axis).astype(wire)
        kept = lax.dynamic_index_in_dim(x, bit, axis)
        return kept + lax.ppermute(sent, name, perm).astype(x.dtype)

    turn_perm = [
        (h * 4 + a * 2 + b, a * 4 + h * 2 + b)
        for h in range(2)
        for a in range(2)
        for b in range(2)
    ]
    z1, z0 = place // 2, place % 2

    def turn(x):
        return lax.ppermute(x, ct, turn_perm)

    def pick(x, index, axis):
        return lax.dynamic_index_in_dim(x, index, axis, keepdims=False)

    def in_order(bit, mine, got):
        return jnp.where(bit == 0, mine, got), jnp.where(bit == 0, got, mine)

    def after(x, *others):
        return lax.optimization_barrier((x, *others))[0]

    def gather_z0(x):
        return in_order(z0, x, lax.ppermute(x, *step_z0[:2]))

    def row_steps(order):
        bits = list(range(pair_bits))
        return [(steps_pair[b], pair_bits - 1 - b) for b in (bits if order == 0 else bits[::-1])]

    def scatter_start(x):
        return x.reshape((2,) * pair_bits + (2, rows, x.shape[-1]))

    def scatter_columns(x, column_pieces):
        sides = [
            jnp.concatenate(
                [
                    x[:, :, (2 * i + side) * column_pieces : (2 * i + side + 1) * column_pieces]
                    for i in range(x.shape[-1] // (2 * column_pieces))
                ],
                axis=-1,
            )
            for side in range(2)
        ]
        return fold(jnp.stack(sides), step_z0, 0)[0]

    def natural(left, right, column_pieces):
        return jnp.concatenate(
            [
                piece[..., i * column_pieces : (i + 1) * column_pieces]
                for i in range(left.shape[-1] // column_pieces)
                for piece in (left, right)
            ],
            axis=-1,
        )

    def bring_z0(x):
        got = lax.ppermute(pick(x, 1 - z0, 0), *step_z0[:2])
        return jnp.concatenate(in_order(z0, pick(x, z0, 0), got), axis=0)

    def both_cores(own):
        return jnp.concatenate(in_order(core, own, swap_core(own)), axis=0)

    def send_back(own):
        x = own.reshape(2, quarter, width)
        got = lax.ppermute(pick(x, 1 - z0, 0), *step_z0[:2])
        return turn(jnp.stack(in_order(z0, pick(x, z0, 0), got)))

    seg_other = swap_core(segment_ids)
    seg_row = lax.dynamic_index_in_dim(
        jnp.where(core == z1, segment_ids, seg_other), z0, 0, keepdims=False
    )
    kseg, qseg = seg_row[:, None], seg_row[None, :]

    def time_forward(steps_all):
        features = step_features(steps_all.reshape(-1))
        hidden_in = matmul_high(features, time_weight1.astype(F32)) + time_bias1.astype(F32)
        gate = 1.0 / (1.0 + jnp.exp(-hidden_in))
        hidden = hidden_in * gate
        partial = matmul_high(hidden, time_weight2.astype(F32))
        own_shift = lax.dynamic_update_slice(
            jnp.zeros((width,), F32), time_bias2.astype(F32), (dp_index * rows,)
        )
        partial = (partial + own_shift).reshape((2,) * pair_bits + (2 * micro, width))
        return features, hidden_in, gate, hidden, partial

    assert units == own_width * 2 and 6 * rows + shard_cols <= units
    chunk_width = units
    small = jnp.concatenate(
        [
            jnp.stack([out_bias, ln1_gain, ln1_bias, ffn_out_bias, ln2_gain, ln2_bias]).reshape(-1),
            q_bias,
            jnp.zeros((chunk_width - 6 * rows - shard_cols,), BF),
            v_bias,
            jnp.zeros((chunk_width - shard_cols,), BF),
            ffn_in_bias,
        ]
    ).reshape(3, chunk_width)
    attn_shard = jnp.concatenate(
        [qkv_weight[0], qkv_weight[1], qkv_weight[2], out_weight.T], axis=1
    )
    attn_shard = jnp.concatenate([attn_shard, jnp.pad(small, ((0, 13), (0, 0)))], axis=0)

    ts = timesteps.astype(F32).reshape((1,) * (1 + pair_bits) + (micro,))
    attn = turn(attn_shard)
    ts = grow(ts, step_core, pair_bits)
    attn, ts = lax.optimization_barrier((attn, ts))
    attn = grow(attn[None], step_z1, 0)
    ts = grow(ts, steps_pair[0], pair_bits - 1)
    ffn = jnp.concatenate([ffn_in_weight, ffn_out_weight.T], axis=1)
    attn, ts, tokens, ffn = lax.optimization_barrier((attn, ts, tokens_in, ffn))
    left, right = gather_z0(attn)
    for b in range(1, pair_bits):
        ts = grow(ts, steps_pair[b], pair_bits - 1 - b)
    tokens = turn(tokens)
    ffn = turn(ffn)
    attn = jnp.concatenate(
        [
            natural(left[:, :rows], right[:, :rows], shard_cols),
            jnp.concatenate([left[:, rows:], right[:, rows:]], axis=-1),
        ],
        axis=1,
    )
    attn, ts = lax.optimization_barrier((attn, ts))
    features, hidden_in, gate, hidden, partial = time_forward(ts)
    lead = (1,) * pair_bits
    attn_a = attn[:, :, :chunk_width].reshape(lead + (2, -1, chunk_width))
    attn_b = attn[:, :, chunk_width:].reshape(lead + (2, -1, chunk_width))
    fold_steps = [(steps_pair[b], pair_bits - 1 - b) for b in reversed(range(pair_bits))]
    for index in range(pair_bits):
        attn_a = grow(attn_a, *row_steps(0)[index])
        attn_b = grow(attn_b, *row_steps(1)[index])
        partial = fold(partial, *fold_steps[index], wire=F32)
        if index == pair_bits - 2 or pair_bits == 1:
            tokens = bring_z0(tokens)
        attn_a, attn_b, partial = lax.optimization_barrier((attn_a, attn_b, partial))
    partial = partial.reshape(2 * micro, width)
    embedded = lax.dynamic_index_in_dim(partial + swap_core(partial), place, 0, keepdims=True)
    tokens = both_cores(tokens)
    ffn = grow(ffn[None], step_z1, 0)
    attn_a = attn_a.reshape((dp_count,) + attn_a.shape[pair_bits + 1 :])
    attn_b = attn_b.reshape((dp_count,) + attn_b.shape[pair_bits + 1 :])
    w_qk = attn_a[:, :rows].reshape(width, chunk_width)
    w_vo = attn_b[:, :rows].reshape(width, chunk_width)
    w_v, w_o = w_vo[:, :own_width], w_vo[:, own_width:]

    small_a = attn_a[:, rows : rows + 3].astype(F32)
    small_b = attn_b[0, rows : rows + 3].astype(F32)
    vectors = (
        small_a[:, 0, : 6 * rows].reshape(dp_count, 6, rows).transpose(1, 0, 2).reshape(6, width)
    )
    out_shift, gain_one, shift_one, ffn_shift, gain_two, shift_two = [vectors[i] for i in range(6)]
    small_z = (small_a[0], small_b)
    own_q_bias = jnp.concatenate([x[0, 6 * rows : 6 * rows + shard_cols] for x in small_z])
    own_v_bias = jnp.concatenate([x[1, :shard_cols] for x in small_z])
    own_in_bias = jnp.concatenate([x[2] for x in small_z])

    attend, attend_back = attention_calls(seq_len, own_width, 256)
    start = tokens.astype(F32) + embedded
    start_low = start.astype(BF)
    shift_qk = jnp.concatenate([own_q_bias, jnp.zeros_like(own_q_bias)])
    qk = (nn(start_low, w_qk) + shift_qk).astype(BF)
    v = (nn(start_low, w_v) + own_v_bias).astype(BF)
    ahead = []
    for i in range(len(attend)):
        filled = (ahead[-1][0],) if ahead else ()
        ahead.append(attend[i](qk, qk, v, kseg, qseg, *filled))
    ffn = after(ffn, ahead[0][1])
    ffn_left, ffn_right = gather_z0(ffn)
    ffn = natural(ffn_left, ffn_right, units)
    w_in = ffn[:, :, : 2 * units].reshape(lead + (2, rows, 2 * units))
    w_out = ffn[:, :, 2 * units :].reshape(lead + (2, rows, 2 * units))
    for index in range(pair_bits):
        if index == 0:
            w_in, w_out = lax.optimization_barrier((w_in, w_out, ahead[1][1]))[:2]
        w_in = grow(w_in, *row_steps(0)[index])
        w_out = grow(w_out, *row_steps(1)[index])
    above = bring_z0(turn(after(cotangent, ahead[-1][1])))
    w_in = w_in.reshape(width, 2 * units)
    w_out = w_out.reshape(width, 2 * units)
    context = ahead[-1][0]
    attended = nt(context, w_o)
    attended = attended + swap_core(attended.astype(BF)).astype(F32)
    xh_one, r_one = norm_parts(start + (attended + out_shift))
    normed = xh_one * gain_one + shift_one
    normed_low = normed.astype(BF)
    inner = nn(normed_low, w_in) + own_in_bias
    activated = gelu_pair(inner)[0].astype(BF)
    branch = nt(activated, w_out)
    branch = branch + swap_core(branch.astype(BF)).astype(F32)
    xh_two, r_two = norm_parts(normed + (branch + ffn_shift))
    half_len = seq_len // 2

    def half_of(x, which):
        return lax.dynamic_slice_in_dim(x, which * half_len, half_len, axis=0)

    output = send_back(half_of((xh_two * gain_two + shift_two).astype(BF), core))

    above = both_cores(above).astype(F32)
    final_grad, gain_two_grad, shift_two_grad = norm_backward(above, xh_two, r_two, gain_two)
    final_low = final_grad.astype(BF)
    ffn_shift_grad = jnp.sum(final_low.astype(F32), axis=0)
    inner_grad = (nn(final_low, w_out) * gelu_slope(inner)).astype(BF)
    in_shift_grad = jnp.sum(inner_grad.astype(F32), axis=0)
    normed_part = nt(inner_grad, w_in)
    normed_other = swap_core(normed_part.astype(BF))
    rows_out = scatter_start(tn(final_low, activated))
    rows_out = fold(rows_out, *row_steps(1)[::-1][0])
    rows_in = scatter_start(tn(normed_low, inner_grad))
    rows_in = fold(rows_in, *row_steps(0)[::-1][0])
    normed_grad = final_grad + normed_part + normed_other.astype(F32)
    mid_grad, gain_one_grad, shift_one_grad = norm_backward(normed_grad, xh_one, r_one, gain_one)
    mid_low = mid_grad.astype(BF)
    out_shift_grad = jnp.sum(mid_low.astype(F32), axis=0)
    context_grad = nn(mid_low, w_o).astype(BF)

    def w_pair(i):
        at = slice(i * 128, (i + 1) * 128)
        return [w_qk[:, :own_width][:, at], w_qk[:, own_width:][:, at], w_v[:, at]]

    grad_o = tn(mid_low, context)
    grads = []
    for i in range(len(attend_back)):
        grads.append(attend_back[i](qk, qk, v, context_grad, ahead[i][1], kseg, qseg))
    rows_in, rows_out = lax.optimization_barrier((rows_in, rows_out, grads[0]))[:2]
    for index in range(1, pair_bits):
        rows_out = fold(rows_out, *row_steps(1)[::-1][index])
        rows_in = fold(rows_in, *row_steps(0)[::-1][index])
    rest = jnp.concatenate(
        [x.reshape(x.shape[pair_bits:]) for x in (rows_in, rows_out)], axis=-1
    )
    rest = after(rest, grads[1])
    rest = scatter_columns(rest, units)
    rest = after(rest, grads[-1])
    rest = fold(rest, step_z1, 0)[0].astype(BF)
    pairs = len(grads)
    d_first, d_last = jnp.concatenate(grads[:-1], axis=1), grads[-1]
    w_first = jnp.concatenate([piece for i in range(pairs - 1) for piece in w_pair(i)], axis=1)
    w_last = jnp.concatenate(w_pair(pairs - 1), axis=1)
    rows_a = fold(scatter_start(tn(start_low, d_first)), *row_steps(0)[::-1][0])
    rows_b = scatter_start(jnp.concatenate([tn(start_low, d_last), grad_o], axis=1))
    rows_b = fold(rows_b, *row_steps(1)[::-1][0])
    start_first = nt(d_first, w_first)
    column_sums = jnp.concatenate(
        [jnp.sum(x.astype(F32), axis=0) for x in (d_first, d_last)]
    ).reshape(pairs, 3, 128)
    q_shift_grad = column_sums[:, 0].reshape(-1)
    v_shift_grad = column_sums[:, 2].reshape(-1)

    start_part = start_first + nt(d_last, w_last)
    start_other = swap_core(half_of(start_part.astype(BF), 1 - core))
    start_grad = half_of(mid_grad, core) + half_of(start_part, core) + start_other.astype(F32)

    def sum_step(x, step):
        return x + lax.ppermute(x, *step[:2])

    first_core = (core == 0).astype(F32)
    tensor_part = jnp.concatenate(
        [
            q_shift_grad.reshape(2, shard_cols),
            v_shift_grad.reshape(2, shard_cols),
            in_shift_grad.reshape(2, units),
        ],
        axis=1,
    )
    tensor_rows = lax.dynamic_update_slice(
        jnp.zeros((4, tensor_part.shape[1]), F32), tensor_part, (2 * core, 0)
    )
    vector_part = first_core * jnp.stack(
        [
            out_shift_grad,
            gain_one_grad,
            shift_one_grad,
            ffn_shift_grad,
            gain_two_grad,
            shift_two_grad,
        ]
    )
    seq_count = micro * dp_count
    time_rows = lax.dynamic_update_slice(
        jnp.zeros((seq_count, width), F32),
        jnp.sum(start_grad, axis=0)[None],
        (pair * 4 + place, 0),
    )
    packed = jnp.concatenate(
        [vector_part.reshape(-1), time_rows.reshape(-1), tensor_rows.reshape(-1)]
    ).reshape(-1, 128)
    rows_a, rows_b, start_grad_low = lax.optimization_barrier(
        (rows_a, rows_b, start_grad.astype(BF))
    )
    packed = sum_step(packed, step_core)
    for index in range(1, pair_bits):
        rows_a = fold(rows_a, *row_steps(0)[::-1][index])
        rows_b = fold(rows_b, *row_steps(1)[::-1][index])
        if index == 1:
            packed = sum_step(packed, step_z0)
        rows_a, rows_b, packed = lax.optimization_barrier((rows_a, rows_b, packed))
    shard_attn = jnp.concatenate(
        [x.reshape(x.shape[pair_bits:]) for x in (rows_a, rows_b)], axis=-1
    )
    by_pair = shard_attn[..., : 3 * own_width]
    shard_attn = jnp.concatenate(
        [
            by_pair[..., (3 * i + part) * 128 : (3 * i + part + 1) * 128]
            for part in range(3)
            for i in range(pairs)
        ]
        + [shard_attn[..., 3 * own_width :]],
        axis=-1,
    )
    shard_attn = scatter_columns(shard_attn, shard_cols)
    packed = sum_step(packed, step_z1)
    shard_attn, packed = lax.optimization_barrier((shard_attn, packed))
    shard_attn = fold(shard_attn, step_z1, 0)[0].astype(BF)
    packed = sum_step(packed, steps_pair[0])
    shard_attn, packed, rest = lax.optimization_barrier((shard_attn, packed, rest))
    finished = turn(jnp.concatenate([rest, shard_attn], axis=1)).astype(F32)
    shard_ffn, shard_attn = finished[:, : 2 * units], finished[:, 2 * units :]
    for step in steps_pair[1:]:
        packed = sum_step(packed, step)
    packed = packed.reshape(-1)
    input_grad = send_back(start_grad_low)
    vector_sums = packed[: 6 * width].reshape(6, width)
    time_sums = packed[6 * width : (6 + seq_count) * width].reshape(seq_count, width)
    tensor_sums = lax.dynamic_index_in_dim(
        packed[(6 + seq_count) * width :].reshape(4, -1), place, 0, keepdims=False
    )
    vector_own = lax.dynamic_slice(vector_sums, (0, dp_index * rows), (6, rows))
    q_total = tensor_sums[:shard_cols]
    v_total = tensor_sums[shard_cols : 2 * shard_cols]
    in_total = tensor_sums[2 * shard_cols :]

    highest_tn = functools.partial(
        lax.dot_general, precision=highest, preferred_element_type=F32
    )
    time_two_grad = highest_tn(hidden, time_sums, (((0,), (0,)), ((), ())))
    hidden_grad = highest_tn(time_sums, time_weight2.astype(F32), (((1,), (1,)), ((), ())))
    pre_grad = hidden_grad * (gate * (1.0 + hidden_in * (1.0 - gate)))
    time_one_grad = highest_tn(features, pre_grad, (((0,), (0,)), ((), ())))
    time_shift_one = jnp.sum(pre_grad, axis=0)
    time_shift_two = lax.dynamic_slice(jnp.sum(time_sums, axis=0), (dp_index * rows,), (rows,))

    return (
        output,
        input_grad,
        jnp.stack([shard_attn[:, i * shard_cols : (i + 1) * shard_cols] for i in range(3)]),
        q_total,
        v_total,
        shard_attn[:, 3 * shard_cols :].T,
        vector_own[0],
        vector_own[1],
        vector_own[2],
        shard_ffn[:, :units],
        in_total,
        shard_ffn[:, units:].T,
        vector_own[3],
        vector_own[4],
        vector_own[5],
        time_one_grad,
        time_shift_one,
        time_two_grad,
        time_shift_two,
    )


def solution(mesh):
    return layer(mesh)


def layer(mesh):
    dp_count, tensor_count = mesh.devices.shape
    assert tensor_count == 4
    pair_count = dp_count // 2
    split = Mesh(
        mesh.devices.reshape(pair_count, 2, tensor_count), ("pair", "core", "tensor")
    )
    dp = ("pair", "core")
    return jax.shard_map(
        functools.partial(local, pair_count),
        mesh=split,
        in_specs=(
            P(dp, "tensor", None),
            P(dp, None),
            P(dp),
            P(dp, "tensor", None),
            P(None, dp, "tensor"),
            P("tensor"),
            P("tensor"),
            P("tensor", dp),
            P(dp),
            P(dp),
            P(dp),
            P(dp, "tensor"),
            P("tensor"),
            P("tensor", dp),
            P(dp),
            P(dp),
            P(dp),
            P(None, dp),
            P(dp),
            P(dp, None),
            P(dp),
        ),
        out_specs=(
            P(dp, "tensor", None),
            P(dp, "tensor", None),
            P(None, dp, "tensor"),
            P("tensor"),
            P("tensor"),
            P("tensor", dp),
            P(dp),
            P(dp),
            P(dp),
            P(dp, "tensor"),
            P("tensor"),
            P("tensor", dp),
            P(dp),
            P(dp),
            P(dp),
            P(None, dp),
            P(dp),
            P(dp, None),
            P(dp),
        ),
        check_vma=False,
    )
```
